32 devices in a mesh: layer: 4 (over x, core), tile: 8 (over z, y).
Axes of the slice: x: 2, y: 2, z: 4, core: 2. Of those that a mesh axis runs over, the one named last changes fastest.
Arguments:
- screens: bfloat16 [12, 8192, 10240], P('layer', 'tile'), may hold values from -5 to 5
- chosen: int32 [8], P('layer'), may hold values from 0 to 2
- row_shift: int32 [8], P('layer'), may hold values from 0 to 1023, as said below
- column_shift: int32 [8], P('layer'), may hold values from 0 to 1920, as said below
- fractions: float32 [8, 2], P('layer'), may hold values from 0 to 1
- pistons: float32 [798], replicated, may hold values from -3 to 3
- segment_map: int32 [32, 32], replicated, may hold values from 0 to 797
- amplitude: bfloat16 [8192, 8192], P('tile'), may hold values from 0 to 10
Outputs:
- intensity: float32 [8192, 8192], P('tile', 'layer')
The draws below stay inside these ranges and needn't reach their ends.
Inputs may be any that keep to these rules, and one draw needn't show every extreme that they name: Entry s takes one of its own group's screens: stored screen (s // 2) * 3 + chosen[s]. `row_shift`: both ends of the range are taken in every draw. `column_shift`: both ends of the range are taken in every draw.
All inputs are finite; a program needn't handle non-finite values.
Results may differ from the reference program's by a relative error of at most 0.0003.
Values may be sent and summed in bfloat16 or wider, within the bound.
No kernel may reach another device: no remote copies, remote signals or barrier semaphores. Data moves between devices by JAX's collectives and lax.ppermute only.
A program may use at most 576 MiB of HBM per device.

```python
import math
import jax
import jax.numpy as jnp
from jax import lax

PUPIL = 8192
PADDED = 16384
SCREEN = 10240
GROUP_LAYERS = 3
PICKED = 2
SEGMENTS = 798
SEG_GRID = 32
DOT_RADIUS = 2
ROWS_DEV = 1024
STORED = 12
PICKED_ALL = 8


def shifts_within(key, count, bound):
    first, second = jax.random.split(key)
    values = jax.random.randint(first, (count,), 0, bound + 1, jnp.int32)
    order = jax.random.permutation(second, count)
    return values.at[order[0]].set(bound).at[order[1]].set(0)


def draw_row_shift(key, part):
    return shifts_within(jax.random.fold_in(key, 11), PICKED_ALL, ROWS_DEV - 1)


def draw_column_shift(key, part):
    return shifts_within(jax.random.fold_in(key, 23), PICKED_ALL, SCREEN - PUPIL - 128)


def draw_screens(key, part):
    keys = jax.random.split(jax.random.fold_in(key, 51), 5)
    shape = (STORED, PUPIL, SCREEN)
    speckle = jnp.clip(jax.random.normal(keys[0], shape, jnp.float32) * 0.6, -3.0, 3.0)
    height = jax.random.uniform(keys[1], (STORED, 1, 1), jnp.float32, 0.5, 1.0)
    period = jnp.exp(jax.random.uniform(keys[2], (STORED, 1, 1), jnp.float32, math.log(PUPIL / 4.0), math.log(float(PUPIL))))
    heading = jax.random.uniform(keys[3], (STORED, 1, 1), jnp.float32, 0.0, 2.0 * math.pi)
    offset = jax.random.uniform(keys[4], (STORED, 1, 1), jnp.float32, 0.0, 2.0 * math.pi)
    row_place = jnp.arange(PUPIL, dtype=jnp.float32)[None, :, None]
    column_place = jnp.arange(SCREEN, dtype=jnp.float32)[None, None, :]
    argument = 2.0 * math.pi / period * (jnp.cos(heading) * row_place + jnp.sin(heading) * column_place) + offset
    smooth = height * jnp.sin(argument)
    return jnp.clip(speckle + smooth, -5.0, 5.0).astype(jnp.bfloat16)


def draw_amplitude(key, part):
    first, second, third = jax.random.split(jax.random.fold_in(key, 37), 3)
    reach = 0.5 * math.log(10.0)
    base = jnp.exp(jax.random.uniform(first, (PUPIL, PUPIL), jnp.float32, math.log(0.1), 0.0))
    row_scale = jnp.exp(jax.random.uniform(second, (PUPIL, 1), jnp.float32, -reach, reach))
    column_scale = jnp.exp(jax.random.uniform(third, (1, PUPIL), jnp.float32, -reach, reach))
    return (base * row_scale * column_scale).astype(jnp.bfloat16)


def with_ends(entries, stream_key, low, largest):
    shape = entries.shape
    index_at = [jax.random.randint(jax.random.fold_in(stream_key, axis), (), 0, shape[axis]) for axis in range(len(shape))]
    entries = entries.at[tuple(index_at)].set(low)
    longest = shape.index(max(shape))
    index_at[longest] = (index_at[longest] + 1) % shape[longest]
    return entries.at[tuple(index_at)].set(largest)


def level_of(own_key, shape, cuts, smallest, top_value):
    def one(position, blocks):
        draws = jax.random.uniform(jax.random.fold_in(jax.random.fold_in(own_key, 6), position), (blocks,), jnp.float32, smallest / len(cuts), top_value / len(cuts))
        return jnp.repeat(jnp.exp(draws), shape[position] // blocks).reshape((-1,) + (1,) * (len(shape) - position - 1))

    loudness = one(*cuts[0])
    for cut in cuts[1:]:
        loudness = loudness * one(*cut)
    return loudness


def centred(stream_key, extent, scale, most, held_as=jnp.bfloat16):
    array = jax.random.normal(stream_key, extent, jnp.float32) * scale
    return jnp.minimum(jnp.maximum(array, -most), most).astype(held_as)


def setup_inputs(seed: int = 0) -> dict:
    splits = jax.random.split(jax.random.key(seed), 9)
    screens = draw_screens(jax.random.fold_in(splits[8], 71), 0)
    chosen = with_ends(jax.random.randint(splits[1], (PICKED_ALL,), 0, GROUP_LAYERS), jax.random.fold_in(splits[1], 1), 0, GROUP_LAYERS - 1).astype(jnp.int32)
    row_shift = draw_row_shift(jax.random.fold_in(splits[8], 71), 0)
    column_shift = draw_column_shift(jax.random.fold_in(splits[8], 71), 0)
    fractions = jnp.clip(1.0 * jax.random.uniform(splits[4], (PICKED_ALL, 2), jnp.float32) ** level_of(splits[4], (PICKED_ALL, 2), ((0, 4),), -0.2, 0.2), 0.0, 1.0)
    pistons = centred(splits[5], (SEGMENTS,), 0.5, 3.0, jnp.float32)
    segment_map = with_ends(jax.random.randint(splits[6], (SEG_GRID, SEG_GRID), 0, SEGMENTS), jax.random.fold_in(splits[6], 1), 0, SEGMENTS - 1).astype(jnp.int32)
    amplitude = draw_amplitude(jax.random.fold_in(splits[8], 71), 0)
    return dict(screens=screens, chosen=chosen, row_shift=row_shift, column_shift=column_shift, fractions=fractions, pistons=pistons, segment_map=segment_map, amplitude=amplitude)


phase_step = math.pi / 2
highest = lax.Precision.HIGHEST


def layer_phase(screen, rows_ahead, columns_ahead, frac_row, frac_column):
    wide = lax.dynamic_slice_in_dim(screen, columns_ahead, PUPIL + 1, 1).astype(jnp.float32)
    across = (1.0 - frac_column) * wide[:, :PUPIL] + frac_column * wide[:, 1:]
    rolled = jnp.roll(across, -rows_ahead, axis=0)
    return (1.0 - frac_row) * rolled + frac_row * jnp.roll(rolled, -1, axis=0)


def dot_table(positions):
    frequency = jnp.arange(2 * DOT_RADIUS + 1, dtype=jnp.int32) - DOT_RADIUS
    steps = (frequency[:, None] * positions[None, :]) % PADDED
    angle = (-2.0 * math.pi / PADDED) * steps.astype(jnp.float32)
    return jnp.cos(angle), jnp.sin(angle)


def complex_einsum(form, first_pair, second_pair):
    real = jnp.einsum(form, first_pair[0], second_pair[0], precision=highest) - jnp.einsum(form, first_pair[1], second_pair[1], precision=highest)
    imaginary = jnp.einsum(form, first_pair[0], second_pair[1], precision=highest) + jnp.einsum(form, first_pair[1], second_pair[0], precision=highest)
    return real, imaginary


def reference(screens, chosen, row_shift, column_shift, fractions, pistons, segment_map, amplitude):
    phase = jnp.zeros((PUPIL, PUPIL), jnp.float32)
    for entry in range(PICKED_ALL):
        group = entry // PICKED
        which = (group * GROUP_LAYERS + chosen[entry]).astype(jnp.int32)
        screen = lax.dynamic_index_in_dim(screens, which, 0, keepdims=False)
        phase = phase + layer_phase(screen, row_shift[entry], column_shift[entry], fractions[entry, 0], fractions[entry, 1])
    grid = jnp.take(pistons, segment_map)
    block = PUPIL // SEG_GRID
    phase = phase + jnp.repeat(jnp.repeat(grid, block, axis=0), block, axis=1)
    magnitude = amplitude.astype(jnp.float32)
    field = (magnitude * jnp.cos(phase), magnitude * jnp.sin(phase))
    table = dot_table(jnp.arange(PUPIL, dtype=jnp.int32))
    half = complex_einsum("fc,rc->fr", table, field)
    coefficient = complex_einsum("gr,fr->gf", table, half)
    frequency = jnp.arange(2 * DOT_RADIUS + 1, dtype=jnp.int32) - DOT_RADIUS
    inside = ((frequency[:, None] ** 2 + frequency[None, :] ** 2) <= DOT_RADIUS ** 2).astype(jnp.float32) / (PADDED * PADDED)
    turn_real = (math.cos(phase_step) - 1.0) * inside
    turn_imaginary = math.sin(phase_step) * inside
    weights = (coefficient[0] * turn_real - coefficient[1] * turn_imaginary, coefficient[0] * turn_imaginary + coefficient[1] * turn_real)
    conjugate = (table[0], -table[1])
    wave = complex_einsum("gf,fc->gc", weights, conjugate)
    wave = complex_einsum("gr,gc->rc", conjugate, wave)
    real = field[0] + wave[0]
    imaginary = field[1] + wave[1]
    return real * real + imaginary * imaginary
```

```python
import functools
import math

import jax
import jax.numpy as jnp
import numpy as np
from jax import lax
from jax.experimental import pallas as pl
from jax.experimental.pallas import tpu as pltpu
from jax.sharding import PartitionSpec as P

DOT_RADIUS = 2
LANES = 128
STEP_INVERSE = 819.0
BASIS = 2 * DOT_RADIUS + 1
CHUNKS = 2
ROW_BLOCK = 32
GROUP = 256


def exchanged(value, axis, bit):
    devices = lax.axis_size(axis)
    return lax.ppermute(value, axis, [(i, i ^ bit) for i in range(devices)])


def handed_back(value):
    devices = lax.axis_size("tile")
    return lax.ppermute(value, "tile", [(i, (i - 1) % devices) for i in range(devices)])


def phase_kernel(plan, chosen, row_shift, column_shift, bases, fractions, screens, *rest):
    picked, rows, strip, first_member, offset, strips, total, adds = plan
    if adds:
        lent_in, mine_in, lent, mine, wide, weights, across, sems = rest
    else:
        lent, mine, wide, weights, across, sems = rest
    groups = strip // GROUP
    pad = ROW_BLOCK + 8
    step = pl.program_id(0) * strips + pl.program_id(1)

    def fetches(position, slot):
        block, part = position // strips, position % strips
        column = bases[first_member + 2 * block] + offset + part * strip
        result = []
        for entry in range(picked):
            start = pl.multiple_of(column + (column_shift[entry] >> 7) * LANES, LANES)
            source = screens.at[chosen[entry], :, pl.ds(start, strip + LANES)]
            result.append(pltpu.make_async_copy(source, wide.at[slot, entry], sems.at[slot, entry]))
        return result

    @pl.when(step == 0)
    def _():
        for copy in fetches(0, 0):
            copy.start()
        for entry in range(picked):
            frac = fractions[entry, 1]
            near = (1.0 - frac) * STEP_INVERSE
            far = frac * STEP_INVERSE
            behind = lax.broadcasted_iota(jnp.int32, (GROUP + LANES, GROUP), 0) - lax.broadcasted_iota(
                jnp.int32, (GROUP + LANES, GROUP), 1
            )
            rest_shift = column_shift[entry] & (LANES - 1)
            band = jnp.where(behind == rest_shift, near, jnp.where(behind == rest_shift + 1, far, 0.0))
            high = band.astype(jnp.bfloat16)
            low = (band - high.astype(jnp.float32)).astype(jnp.bfloat16)
            weights[entry, 0:GROUP, :] = high[:GROUP]
            weights[entry, GROUP : 2 * GROUP, :] = low[:GROUP]
            weights[entry, 2 * GROUP : 2 * GROUP + LANES, :] = high[GROUP:]
            weights[entry, 2 * GROUP + LANES :, :] = low[GROUP:]
            for lane_tile in range(2 * groups):
                across[entry, lane_tile, :pad, :] = jnp.zeros((pad, LANES), jnp.float32)
                across[entry, lane_tile, pad + rows :, :] = jnp.zeros((pad, LANES), jnp.float32)

    slot = step % 2

    @pl.when(step + 1 < total)
    def _():
        for copy in fetches(step + 1, 1 - slot):
            copy.start()

    for copy in fetches(step, slot):
        copy.wait()

    row_chunk = min(256, rows)
    for entry in range(picked):

        @pl.loop(0, rows // row_chunk)
        def _(chunk):
            first = pl.multiple_of(chunk * row_chunk, row_chunk)
            for group in range(groups):
                left = group * GROUP
                body = wide[slot, entry, pl.ds(first, row_chunk), left : left + GROUP]
                tail = wide[slot, entry, pl.ds(first, row_chunk), left + GROUP : left + GROUP + LANES]
                mixed = jnp.dot(
                    jnp.concatenate([body, body, tail, tail], axis=1),
                    weights[entry],
                    preferred_element_type=jnp.float32,
                )
                across[entry, 2 * group, pl.ds(pad + first, row_chunk), :] = mixed[:, :LANES]
                across[entry, 2 * group + 1, pl.ds(pad + first, row_chunk), :] = mixed[:, LANES:]

    far_weight = [fractions[entry, 0] for entry in range(picked)]
    near_weight = [1.0 - far_weight[entry] for entry in range(picked)]

    def windows(out, added, origin):
        @pl.loop(0, rows // ROW_BLOCK)
        def _(block):
            first = pl.multiple_of(block * ROW_BLOCK, ROW_BLOCK)
            starts = [
                pad + jnp.clip(first + origin + row_shift[entry], -(ROW_BLOCK + 1), rows)
                for entry in range(picked)
            ]
            for lane_tile in range(2 * groups):
                lanes = slice(lane_tile * LANES, (lane_tile + 1) * LANES)
                value = None
                for entry in range(picked):
                    near = across[entry, lane_tile, pl.ds(starts[entry], ROW_BLOCK), :]
                    far = across[entry, lane_tile, pl.ds(starts[entry] + 1, ROW_BLOCK), :]
                    term = near_weight[entry] * near + far_weight[entry] * far
                    value = term if value is None else value + term
                count = jnp.round(value).astype(jnp.int32)
                if added is not None:
                    count = count + added[0, pl.ds(first, ROW_BLOCK), lanes].astype(jnp.int32)
                out[0, pl.ds(first, ROW_BLOCK), lanes] = count.astype(jnp.int16)

    windows(lent, lent_in if adds else None, -rows)
    windows(mine, mine_in if adds else None, 0)


def group_phase(args, bases, first_member, blocks, offset, width, added=None, added_block=0):
    screens, chosen, row_shift, column_shift, fractions = args
    picked = chosen.shape[0]
    rows = screens.shape[1]
    strip = min(2 * GROUP, width)
    strips = width // strip
    pad = ROW_BLOCK + 8
    plan = (picked, rows, strip, first_member, offset, strips, blocks * strips, added is not None)
    tile = pl.BlockSpec((1, rows, strip), lambda b, s, *_: (b, 0, s))
    in_specs = [pl.BlockSpec(memory_space=pltpu.SMEM), pl.BlockSpec(memory_space=pl.ANY)]
    operands = [fractions, screens]
    if added is not None:
        received = pl.BlockSpec((1, rows, strip), lambda b, s, *_: (b + added_block, 0, s))
        in_specs += [received, received]
        operands += list(added)
    shape = jax.ShapeDtypeStruct((blocks, rows, width), jnp.int16)
    cells = blocks * rows * width
    return pl.pallas_call(
        functools.partial(phase_kernel, plan),
        out_shape=(shape, shape),
        grid_spec=pltpu.PrefetchScalarGridSpec(
            num_scalar_prefetch=4,
            grid=(blocks, strips),
            in_specs=in_specs,
            out_specs=(tile, tile),
            scratch_shapes=[
                pltpu.VMEM((2, picked, rows, strip + LANES), jnp.bfloat16),
                pltpu.VMEM((picked, 2 * (GROUP + LANES), GROUP), jnp.bfloat16),
                pltpu.VMEM((picked, strip // LANES, rows + 2 * pad, LANES), jnp.float32),
                pltpu.SemaphoreType.DMA((2, picked)),
            ],
        ),
        compiler_params=pltpu.CompilerParams(dimension_semantics=("arbitrary", "arbitrary")),
        cost_estimate=pl.CostEstimate(
            flops=cells * picked * 4 * GROUP, bytes_accessed=cells * 12, transcendentals=0
        ),
        name="group_phase",
    )(chosen, row_shift, column_shift, bases, *operands)


def fitted(function, odd):
    places = 0.5 * np.cos(np.pi * (np.arange(400) + 0.5) / 800)
    squares = places * places
    wanted = function(np.pi * places) / (places if odd else 1.0)
    powers = np.stack([squares**k for k in range(6)], axis=1)
    scale = places if odd else np.ones_like(places)
    found = np.linalg.lstsq(powers * scale[:, None], wanted * scale, rcond=None)[0]
    return [float(np.float32(value)) for value in found]


SINE = fitted(np.sin, True)
COSINE = fitted(np.cos, False)


def horner(coefficients, x):
    value = jnp.full_like(x, coefficients[-1])
    for coefficient in coefficients[-2::-1]:
        value = value * x + coefficient
    return value


def field_kernel(plan, place, pistons, first, second, third, amplitude, table, down, *rest):
    rows, offset, cell, aliased = plan
    if aliased:
        rest = rest[2:]
    real, imaginary, sums, parts, half = rest
    part = pl.program_id(0)
    column_cell = (place[1] + offset + part * GROUP) // cell

    @pl.loop(0, rows // ROW_BLOCK)
    def _(block):
        start = pl.multiple_of(block * ROW_BLOCK, ROW_BLOCK)
        here = pl.ds(start, ROW_BLOCK)
        count = (
            first[0, here, :].astype(jnp.int32)
            + second[0, here, :].astype(jnp.int32)
            + third[0, here, :].astype(jnp.int32)
        )
        piston = pistons[(place[0] + start) // cell, column_cell] * (1.0 / math.pi)
        turns = count.astype(jnp.float32) * (1.0 / (STEP_INVERSE * math.pi)) + piston
        whole = jnp.round(turns)
        left = turns - whole
        odd = (whole.astype(jnp.int32) & 1) == 1
        size = amplitude[here, :].astype(jnp.float32)
        size = jnp.where(odd, -size, size)
        square = left * left
        for index, value in ((0, size * horner(COSINE, square)), (1, size * (left * horner(SINE, square)))):
            (real, imaginary)[index][here, :] = value
            high = value.astype(jnp.bfloat16)
            low = (value - high.astype(jnp.float32)).astype(jnp.bfloat16)
            parts[here, 2 * index * GROUP : (2 * index + 1) * GROUP] = high
            parts[here, (2 * index + 1) * GROUP : (2 * index + 2) * GROUP] = low

    @pl.when(part == 0)
    def _():
        half[...] = jnp.zeros_like(half)

    row_chunk = min(256, rows)

    @pl.loop(0, rows // row_chunk)
    def _(chunk):
        here = pl.ds(pl.multiple_of(chunk * row_chunk, row_chunk), row_chunk)
        half[here, :] += jnp.dot(
            parts[here, : 2 * GROUP],
            jnp.concatenate([table[0], table[0]], axis=0),
            preferred_element_type=jnp.float32,
        ) + jnp.dot(
            parts[here, 2 * GROUP :],
            jnp.concatenate([table[1], table[1]], axis=0),
            preferred_element_type=jnp.float32,
        )

    @pl.when(part == pl.num_programs(0) - 1)
    def _():
        sums[...] = jnp.dot(
            down[...], half[...], preferred_element_type=jnp.float32, precision=lax.Precision.HIGHEST
        )


def field_part(place, grid, terms, amplitude, table, down, share, offset, cell, previous):
    rows = amplitude.shape[0]
    width = terms[0][0].shape[2]
    plan = (rows, offset, cell, previous is not None)

    def term(block):
        return pl.BlockSpec((1, rows, GROUP), lambda s, place: (block, 0, s))

    at = offset // GROUP
    in_specs = [pl.BlockSpec(memory_space=pltpu.SMEM)]
    in_specs += [term(block) for _, block in terms]
    in_specs += [
        pl.BlockSpec((rows, GROUP), lambda s, place: (0, place[1] // GROUP + at + s)),
        pl.BlockSpec((2, GROUP, LANES), lambda s, place: (0, at + s, 0)),
        pl.BlockSpec(down.shape, lambda s, place: (0, 0)),
    ]
    operands = [grid, *[value for value, _ in terms], amplitude, table, down]
    aliases = {}
    if previous is not None:
        in_specs += [pl.BlockSpec(memory_space=pl.ANY)] * 2
        aliases = {len(operands) + 1: 0, len(operands) + 2: 1}
        operands += list(previous)
    shape = jax.ShapeDtypeStruct((rows, share), jnp.float32)
    out = pl.BlockSpec((rows, GROUP), lambda s, place: (0, at + s))
    return pl.pallas_call(
        functools.partial(field_kernel, plan),
        out_shape=(shape, shape, jax.ShapeDtypeStruct((8, LANES), jnp.float32)),
        grid_spec=pltpu.PrefetchScalarGridSpec(
            num_scalar_prefetch=1,
            grid=(width // GROUP,),
            in_specs=in_specs,
            out_specs=(out, out, pl.BlockSpec((8, LANES), lambda s, place: (0, 0))),
            scratch_shapes=[
                pltpu.VMEM((rows, 4 * GROUP), jnp.bfloat16),
                pltpu.VMEM((rows, LANES), jnp.float32),
            ],
        ),
        input_output_aliases=aliases,
        compiler_params=pltpu.CompilerParams(dimension_semantics=("arbitrary",)),
        cost_estimate=pl.CostEstimate(
            flops=rows * width * 1000, bytes_accessed=rows * width * 16, transcendentals=0
        ),
        name="field_part",
    )(place, *operands)


def image_kernel(real, imaginary, down, wave, out, spread):
    columns = real.shape[1]

    @pl.when(pl.program_id(0) == 0)
    def _():
        for index in range(2):
            value = wave[index]
            high = value.astype(jnp.bfloat16)
            low = (value - high.astype(jnp.float32)).astype(jnp.bfloat16)
            upper = lax.broadcasted_iota(jnp.int32, value.shape, 0) < 2 * BASIS
            chosen = jnp.where(upper, high.astype(jnp.float32), low.astype(jnp.float32))
            spread[index] = chosen.astype(jnp.bfloat16)

    for left in range(0, columns, GROUP):
        here = slice(left, left + GROUP)
        first = real[:, here] + jnp.dot(down[...], spread[0, :, here], preferred_element_type=jnp.float32)
        second = imaginary[:, here] + jnp.dot(down[...], spread[1, :, here], preferred_element_type=jnp.float32)
        out[:, here] = first * first + second * second


def image(real, imaginary, down, wave):
    rows, columns = real.shape
    block = min(128, rows)
    tile = pl.BlockSpec((block, columns), lambda i: (i, 0))
    return pl.pallas_call(
        image_kernel,
        out_shape=jax.ShapeDtypeStruct((rows, columns), jnp.float32),
        grid=(rows // block,),
        in_specs=[
            tile,
            tile,
            pl.BlockSpec((block, down.shape[1]), lambda i: (i, 0)),
            pl.BlockSpec(wave.shape, lambda i: (0, 0, 0)),
        ],
        out_specs=tile,
        scratch_shapes=[pltpu.VMEM(wave.shape, jnp.bfloat16)],
        compiler_params=pltpu.CompilerParams(dimension_semantics=("arbitrary",)),
        cost_estimate=pl.CostEstimate(
            flops=rows * columns * 100, bytes_accessed=rows * columns * 12, transcendentals=0
        ),
        name="image",
    )(real, imaginary, down, wave)


def basis_table(positions, padded):
    frequency = jnp.arange(1, DOT_RADIUS + 1, dtype=jnp.int32)
    steps = (positions[:, None] * frequency[None, :]) % padded
    angle = (2.0 * math.pi / padded) * steps.astype(jnp.float32)
    ones = jnp.ones((positions.shape[0], 1), jnp.float32)
    return jnp.concatenate([ones, jnp.cos(angle), jnp.sin(angle)], axis=1)


def two_terms(value):
    high = lax.reduce_precision(value, 8, 7)
    low = lax.reduce_precision(value - high, 8, 7)
    return high, low


def weight_map(padded):
    upward = np.zeros((BASIS, BASIS), complex)
    for index in range(BASIS):
        f = index - DOT_RADIUS
        if f == 0:
            upward[index, 0] = 1.0
        else:
            upward[index, abs(f)] = 1.0
            upward[index, DOT_RADIUS + abs(f)] = 1j * np.sign(f)
    f = np.arange(BASIS) - DOT_RADIUS
    inside = (f[:, None] ** 2 + f[None, :] ** 2 <= DOT_RADIUS**2) / float(padded) ** 2
    turn = (np.exp(1j * math.pi / 2) - 1.0) * inside
    downward = np.conj(upward)
    full = np.einsum("ga,fb,gf,gc,fd->abcd", upward, upward, turn, downward, downward)
    table = np.zeros((2, 4 * BASIS, BASIS, 8, LANES), np.float32)
    for repeat in range(4):
        for half in range(2):
            here = slice(repeat * BASIS, (repeat + 1) * BASIS)
            reals = slice(half * BASIS, (half + 1) * BASIS)
            imaginaries = slice((2 + half) * BASIS, (3 + half) * BASIS)
            table[0, here, :, :BASIS, reals] = full.real
            table[0, here, :, :BASIS, imaginaries] = -full.imag
            table[1, here, :, :BASIS, reals] = full.imag
            table[1, here, :, :BASIS, imaginaries] = full.real
    return table


def summed_over_all(value):
    for axis in ("layer", "tile"):
        bit = 1
        while bit < lax.axis_size(axis):
            value = value + exchanged(value, axis, bit)
            bit *= 2
    return value


def body(screens, chosen, row_shift, column_shift, fractions, pistons, segment_map, amplitude):
    rows, pupil = amplitude.shape
    padded = 2 * pupil
    layers = lax.axis_size("layer")
    layer_index = lax.axis_index("layer")
    tile_index = lax.axis_index("tile")
    share = pupil // layers
    cell = pupil // segment_map.shape[0]
    width = share // (2 * CHUNKS)
    args = (screens, chosen, row_shift, column_shift, fractions)
    bases = (layer_index ^ jnp.arange(layers, dtype=jnp.int32)) * share

    labels = jnp.arange(pistons.shape[0], dtype=jnp.int32)
    grid = jnp.sum(jnp.where(segment_map[:, :, None] == labels, pistons, 0.0), axis=2)
    place = jnp.stack([tile_index * rows, layer_index * share]).astype(jnp.int32)

    across = basis_table(layer_index * share + jnp.arange(share, dtype=jnp.int32), padded)
    high, low = two_terms(across)
    empty = jnp.zeros((share, 2 * BASIS), jnp.float32)
    fill = jnp.zeros((share, LANES - 4 * BASIS), jnp.float32)
    table = jnp.stack(
        [
            jnp.concatenate([high, low, empty, fill], axis=1),
            jnp.concatenate([empty, high, low, fill], axis=1),
        ]
    ).astype(jnp.bfloat16)
    down = basis_table(tile_index * rows + jnp.arange(rows, dtype=jnp.int32), padded)
    down_sum = jnp.concatenate([down.T, jnp.zeros((8 - BASIS, rows), jnp.float32)], axis=0)
    high, low = two_terms(down)
    down_wave = jnp.concatenate([high, low, high, low], axis=1).astype(jnp.bfloat16)

    offsets = [(chunk * width, share // 2 + chunk * width) for chunk in range(CHUNKS)]
    sent = []
    for first, second in offsets:
        pairs = []
        for offset in (second, first):
            lent, mine = group_phase(args, bases, 1, 2, offset, width)
            pairs.append((exchanged(lent, "layer", 1), exchanged(mine, "layer", 1)))
        sent.append(pairs[::-1])
    field = None
    sums = None
    parts = []
    for (first, second), (from_first, from_second) in zip(offsets, sent):
        far_lent, far_mine = group_phase(args, bases, 2, 1, second, width, from_second, 1)
        far_lent = exchanged(far_lent, "layer", 2)
        far_mine = exchanged(far_mine, "layer", 2)
        lent, mine = group_phase(args, bases, 0, 2, first, width, from_first, 0)
        lent = handed_back(lent)
        near_lent, near_mine = group_phase(args, bases, 0, 1, second, width, from_second, 0)
        crossed = exchanged(mine[1:] + lent[1:], "layer", 2)
        returned = handed_back(near_lent + far_lent)
        parts.append((first, [(mine, 0), (lent, 0), (crossed, 0)]))
        parts.append((second, [(near_mine, 0), (far_mine, 0), (returned, 0)]))
    for offset, terms in parts:
        *field, partial = field_part(
            place, grid, terms, amplitude, table, down_sum, share, offset, cell, field
        )
        sums = partial if sums is None else sums + partial
    sums = summed_over_all(sums)
    wave = jnp.sum(jnp.asarray(weight_map(padded)) * sums, axis=(3, 4))
    wave = jnp.sum(wave[:, :, :, None] * across.T[None, None], axis=2)
    return image(field[0], field[1], down_wave, wave)


def solution(mesh):
    return jax.shard_map(
        body,
        mesh=mesh,
        in_specs=(
            P("layer", "tile", None),
            P("layer"),
            P("layer"),
            P("layer"),
            P("layer", None),
            P(),
            P(),
            P("tile", None),
        ),
        out_specs=P("tile", "layer"),
        check_vma=False,
    )
```
